32 devices in a mesh: vol: 1, slab: 8 (over z, x), filt: 4 (over y, core).
Axes of the slice: x: 2, y: 2, z: 4, core: 2. Of those that a mesh axis runs over, the one named last changes fastest.
Arguments:
- volume: bfloat16 [32, 64, 64, 256], P(('vol', 'slab', 'filt')), may hold values from -6 to 6
- weights: bfloat16 [256, 27, 256], P('filt'), may hold values from -0.078125 to 0.078125
- bias: bfloat16 [256], P('filt'), may hold values from -3 to 3
Outputs:
- activated: bfloat16 [32, 64, 64, 256], P(('vol', 'slab'), None, None, 'filt')
The draws below stay inside these ranges and needn't reach their ends.
All inputs are finite; a program needn't handle non-finite values.
Results may differ from the reference program's by a relative error of at most 0.001.
Values may be sent and summed in bfloat16 or wider, within the bound.
A program may use at most 448 MiB of HBM per device.

```python
import jax
import jax.numpy as jnp

C = 256
NY = 64
NX = 64
DEPTH = 32


def steps_of(own_key, extent, pieces, low, top_value):
    factor_of = 1.0
    for dim, blocks in pieces:
        heights = jax.random.uniform(jax.random.fold_in(jax.random.fold_in(own_key, 6), dim), (blocks,), jnp.float32, low / len(pieces), top_value / len(pieces))
        factor_of = factor_of * jnp.repeat(jnp.exp(heights), extent[dim] // blocks).reshape((-1,) + (1,) * (len(extent) - 1 - dim))
    return factor_of


def gaussian(rng, dims, deviation, limit, cuts=(), dtype=jnp.bfloat16):
    gain = steps_of(rng, dims, cuts, -0.22, 0.18) if cuts else 1.0
    entries = jax.random.normal(rng, dims, jnp.float32) * deviation * gain
    return jnp.minimum(jnp.maximum(entries, -limit), limit).astype(dtype)


def setup_inputs(seed: int = 0, part: int = 0) -> dict:
    key_of = jax.random.split(jax.random.key(seed), 4)
    part_splits = jax.random.split(jax.random.fold_in(key_of[3], part), 4)
    volume = gaussian(part_splits[0], (DEPTH, NY, NX, C), 1.0, 6.0, ((0, 32),))
    weights = gaussian(key_of[1], (C, 27, C), (27 * C) ** -0.5, 0.078125, ((0, 4),))
    bias = gaussian(key_of[2], (C,), 0.5, 3.0, ((0, 4),))
    return dict(volume=volume, weights=weights, bias=bias)


def reference(volume, weights, bias):
    depth, rows, cols, chans = volume.shape
    outs = weights.shape[0]
    padded = jnp.pad(volume, ((1, 1), (1, 1), (1, 1), (0, 0)))
    total = jnp.zeros((depth, rows * cols, outs), jnp.float32)
    for tap_z in range(3):
        for tap_y in range(3):
            for tap_x in range(3):
                window = padded[tap_z:tap_z + depth, tap_y:tap_y + rows, tap_x:tap_x + cols].reshape(depth, rows * cols, chans)
                tap_weight = weights[:, 9 * tap_z + 3 * tap_y + tap_x, :]
                total = total + jnp.einsum("zpi,oi->zpo", window.astype(jnp.float32), tap_weight.astype(jnp.float32))
    shifted = total + bias.astype(jnp.float32)[None, None, :]
    result = jnp.where(shifted > 0, shifted, 0.3 * shifted)
    return result.astype(jnp.bfloat16).reshape(depth, rows, cols, outs)
```

```python
import functools

import jax
import jax.numpy as jnp
from jax import lax
from jax.experimental import pallas as pl
from jax.experimental.pallas import tpu as pltpu
from jax.sharding import PartitionSpec as P

CHUNKS = 16
MESH = pl.DeviceIdType.MESH


def kernel(slabs, vol_ref, w_ref, b_ref, out_ref, x, matrix, send, recv, local):
    rows, cols, chans = vol_ref.shape[1:]
    outs = out_ref.shape[-1]
    step_rows = rows // CHUNKS
    m = step_rows * cols
    v = lax.axis_index("vol")
    s = lax.axis_index("slab")
    f = lax.axis_index("filt")
    odd = lax.rem(f, 2)
    mate = f + 1 - 2 * odd
    across = lax.rem(f + 2, 4)
    diag = 3 - f
    outer = (f == 0) | (f == 3)
    has_prev = s > 0
    has_next = s < slabs - 1
    is_odd = odd == 1
    halo_to = s + 2 * odd - 1
    halo_slot = 5 - 5 * odd
    mate_slot = 5 * odd
    sends_halo = (is_odd & has_next) | (~is_odd & has_prev)
    takes_halo = (is_odd & has_prev) | (~is_odd & has_next)
    mate_halo = sends_halo

    def span(k):
        lo = 0 if k == 0 else step_rows * k + 1
        hi = rows if k == CHUNKS - 1 else step_rows * (k + 1) + 1
        return lo, hi - lo

    def own(k):
        lo, n = span(k)
        return vol_ref.at[0, pl.ds(lo, n)]

    def slot(z, k):
        lo, n = span(k)
        return x.at[z, pl.ds(lo + 1, n)]

    def remote(src, z, k, kind, dev):
        return pltpu.make_async_remote_copy(
            src_ref=src,
            dst_ref=slot(z, k),
            send_sem=send.at[kind, k],
            recv_sem=recv.at[z, k],
            device_id=dev,
            device_id_type=MESH,
        )

    to_across = (v, s, across)
    to_mate = (v, s, mate)
    to_halo = (v, halo_to, f)

    def c_y(k):
        return remote(own(k), f + 1, k, 0, to_across)

    def c_core(k):
        return remote(own(k), f + 1, k, 1, to_mate)

    def c_fwd(k):
        return remote(slot(across + 1, k), across + 1, k, 2, to_mate)

    def c_halo_own(k):
        return remote(own(k), halo_slot, k, 3, to_halo)

    def c_halo_fwd(k):
        return remote(slot(across + 1, k), halo_slot, k, 3, to_halo)

    def c_halo_mate(k):
        return remote(slot(halo_slot_in, k), halo_slot_in, k, 4, to_mate)

    halo_slot_in = halo_slot

    def c_local(k):
        return pltpu.make_async_copy(own(k), slot(f + 1, k), local.at[k])

    def arrived(z, k):
        remote(slot(z, k), z, k, 0, to_mate).wait_recv()

    barrier = pltpu.get_barrier_semaphore()
    pl.semaphore_signal(barrier, inc=1, device_id=to_mate, device_id_type=MESH)
    pl.semaphore_signal(barrier, inc=1, device_id=to_across, device_id_type=MESH)

    @pl.when(has_prev)
    def _():
        pl.semaphore_signal(barrier, inc=1, device_id=(v, s - 1, f), device_id_type=MESH)

    @pl.when(has_next)
    def _():
        pl.semaphore_signal(barrier, inc=1, device_id=(v, s + 1, f), device_id_type=MESH)

    inner = has_prev & has_next

    @pl.when(inner)
    def _():
        pl.semaphore_wait(barrier, 4)

    @pl.when(~inner)
    def _():
        pl.semaphore_wait(barrier, 3)

    for k in range(CHUNKS):
        c_y(k).start()

        @pl.when(outer & sends_halo)
        def _():
            c_halo_own(k).start()

        c_core(k).start()
        c_local(k).start()

    zero_row = jnp.zeros((cols, chans), x.dtype)
    for z in range(6):
        x[z, 0] = zero_row
        x[z, rows + 1] = zero_row

    def clear(z):
        @pl.loop(1, rows + 1)
        def _(r):
            x[z, r] = zero_row

    @pl.when(~has_prev)
    def _():
        clear(0)

    @pl.when(~has_next)
    def _():
        clear(5)

    for t in range(9):
        left, middle, right = (w_ref[3 * t + i] for i in range(3))
        tap = jnp.concatenate([middle, left, right, jnp.zeros_like(left)], axis=0)
        matrix[chans * t : chans * (t + 1)] = tap.T

    bias = b_ref[...].astype(jnp.float32)
    place = lax.rem(lax.broadcasted_iota(jnp.int32, (m, 2 * outs), 0), cols)

    def compute(k):
        @pl.loop(0, 4)
        def _(z):
            windows = [
                x[z + dz, pl.ds(step_rows * k + dy, step_rows)].reshape(m, chans)
                for dz in range(3)
                for dy in range(3)
            ]
            total = jnp.dot(
                jnp.concatenate(windows, axis=1), matrix[...], preferred_element_type=jnp.float32
            )
            near = total[:, : 2 * outs]
            far = total[:, 2 * outs :]
            before = jnp.where(place == 0, 0.0, pltpu.roll(near, 1, 0))
            after = jnp.where(place == cols - 1, 0.0, pltpu.roll(far, m - 1, 0))
            full = near + after + pltpu.roll(before, outs, 1)
            shifted = full[:, :outs] + bias
            result = jnp.where(shifted > 0, shifted, 0.3 * shifted)
            out_ref[z, pl.ds(step_rows * k, step_rows)] = result.astype(out_ref.dtype).reshape(
                step_rows, cols, outs
            )

    for t in range(CHUNKS + 2):
        k = t
        if k < CHUNKS:
            arrived(across + 1, k)
            c_fwd(k).start()

            @pl.when(~outer & sends_halo)
            def _():
                c_halo_fwd(k).start()

        k = t - 1
        if 0 <= k < CHUNKS:

            @pl.when(takes_halo)
            def _():
                arrived(halo_slot_in, k)
                c_halo_mate(k).start()

        k = t - 2
        if 0 <= k < CHUNKS:
            c_local(k).wait()
            arrived(mate + 1, k)
            arrived(diag + 1, k)

            @pl.when(mate_halo)
            def _():
                arrived(mate_slot, k)

            compute(k)

    for k in range(CHUNKS):
        c_y(k).wait_send()
        c_core(k).wait_send()
        c_fwd(k).wait_send()

        @pl.when(sends_halo)
        def _():
            c_halo_fwd(k).wait_send()

        @pl.when(takes_halo)
        def _():
            c_halo_mate(k).wait_send()


def body(volume, weights, bias):
    planes, rows, cols, chans = volume.shape
    outs = weights.shape[0]
    slabs = lax.axis_size("slab")
    depth = planes * lax.axis_size("filt")
    taps = weights.transpose(1, 0, 2)
    return pl.pallas_call(
        functools.partial(kernel, slabs),
        out_shape=jax.ShapeDtypeStruct((depth, rows, cols, outs), jnp.bfloat16),
        in_specs=[
            pl.BlockSpec(memory_space=pl.ANY),
            pl.BlockSpec(memory_space=pltpu.VMEM),
            pl.BlockSpec(memory_space=pltpu.VMEM),
        ],
        out_specs=pl.BlockSpec(memory_space=pltpu.VMEM),
        scratch_shapes=[
            pltpu.VMEM((depth + 2, rows + 2, cols, chans), jnp.bfloat16),
            pltpu.VMEM((9 * chans, 4 * outs), jnp.bfloat16),
            pltpu.SemaphoreType.DMA((5, CHUNKS)),
            pltpu.SemaphoreType.DMA((6, CHUNKS)),
            pltpu.SemaphoreType.DMA((CHUNKS,)),
        ],
        compiler_params=pltpu.CompilerParams(
            collective_id=0, has_side_effects=True, vmem_limit_bytes=50 * 1024 * 1024
        ),
        cost_estimate=pl.CostEstimate(
            flops=2 * depth * rows * cols * outs * 27 * chans,
            bytes_accessed=16 * rows * cols * chans,
            transcendentals=0,
        ),
    )(volume, taps, bias.reshape(1, outs))


def solution(mesh):
    return jax.shard_map(
        body,
        mesh=mesh,
        in_specs=(P(("vol", "slab", "filt"), None, None, None), P("filt", None, None), P("filt")),
        out_specs=P(("vol", "slab"), None, None, "filt"),
        check_vma=False,
    )
```

```python
import functools

import jax
import jax.numpy as jnp
from jax import lax
from jax.experimental import pallas as pl
from jax.experimental.pallas import tpu as pltpu
from jax.sharding import PartitionSpec as P

ENDS = (10, 20, 30, 39, 47, 54, 59, 62, 64)
CHUNKS = len(ENDS)
MESH = pl.DeviceIdType.MESH


def kernel(slabs, vol_ref, w_hbm, b_hbm, out_ref, x, matrix, w_ref, b_ref, send, recv, local, params):
    rows, cols, chans = vol_ref.shape[1:]
    outs = out_ref.shape[-1]
    ends = [rows * e // ENDS[-1] for e in ENDS]
    begins = [0] + ends[:-1]
    v = lax.axis_index("vol")
    s = lax.axis_index("slab")
    f = lax.axis_index("filt")
    odd = lax.rem(f, 2)
    mate = f + 1 - 2 * odd
    across = lax.rem(f + 2, 4)
    diag = 3 - f
    outer = (f == 0) | (f == 3)
    has_prev = s > 0
    has_next = s < slabs - 1
    is_odd = odd == 1
    halo_to = s + 2 * odd - 1
    halo_slot = 5 - 5 * odd
    mate_slot = 5 * odd
    sends_halo = (is_odd & has_next) | (~is_odd & has_prev)
    takes_halo = (is_odd & has_prev) | (~is_odd & has_next)
    mate_halo = sends_halo

    def span(k):
        lo = 0 if k == 0 else begins[k] + 1
        hi = rows if k == CHUNKS - 1 else ends[k] + 1
        return lo, hi - lo

    def own(k):
        lo, n = span(k)
        return vol_ref.at[0, pl.ds(lo, n)]

    def slot(z, k):
        lo, n = span(k)
        return x.at[z, pl.ds(lo + 1, n)]

    def remote(src, z, k, kind, dev):
        return pltpu.make_async_remote_copy(
            src_ref=src,
            dst_ref=slot(z, k),
            send_sem=send.at[kind, k],
            recv_sem=recv.at[z, k],
            device_id=dev,
            device_id_type=MESH,
        )

    to_across = (v, s, across)
    to_mate = (v, s, mate)
    to_halo = (v, halo_to, f)

    def c_y(k):
        return remote(own(k), f + 1, k, 0, to_across)

    def c_core(k):
        return remote(own(k), f + 1, k, 1, to_mate)

    def c_fwd(k):
        return remote(slot(across + 1, k), across + 1, k, 2, to_mate)

    def c_halo_own(k):
        return remote(own(k), halo_slot, k, 3, to_halo)

    def c_halo_fwd(k):
        return remote(slot(across + 1, k), halo_slot, k, 3, to_halo)

    def c_halo_mate(k):
        return remote(slot(halo_slot_in, k), halo_slot_in, k, 4, to_mate)

    halo_slot_in = halo_slot

    def c_local(k):
        return pltpu.make_async_copy(own(k), slot(f + 1, k), local.at[k])

    def arrived(z, k):
        remote(slot(z, k), z, k, 0, to_mate).wait_recv()

    get_w = pltpu.make_async_copy(w_hbm, w_ref, params.at[0])
    get_b = pltpu.make_async_copy(b_hbm, b_ref, params.at[1])
    get_w.start()
    get_b.start()

    barrier = pltpu.get_barrier_semaphore()
    pl.semaphore_signal(barrier, inc=1, device_id=to_mate, device_id_type=MESH)
    pl.semaphore_signal(barrier, inc=1, device_id=to_across, device_id_type=MESH)

    @pl.when(has_prev)
    def _():
        pl.semaphore_signal(barrier, inc=1, device_id=(v, s - 1, f), device_id_type=MESH)

    @pl.when(has_next)
    def _():
        pl.semaphore_signal(barrier, inc=1, device_id=(v, s + 1, f), device_id_type=MESH)

    inner = has_prev & has_next

    @pl.when(inner)
    def _():
        pl.semaphore_wait(barrier, 4)

    @pl.when(~inner)
    def _():
        pl.semaphore_wait(barrier, 3)

    for k in range(CHUNKS):
        c_y(k).start()

        @pl.when(outer & sends_halo)
        def _():
            c_halo_own(k).start()

        c_core(k).start()
        c_local(k).start()

    zero_row = jnp.zeros((cols, chans), x.dtype)
    for z in range(6):
        x[z, 0] = zero_row
        x[z, rows + 1] = zero_row

    def clear(z):
        @pl.loop(1, rows + 1)
        def _(r):
            x[z, r] = zero_row

    @pl.when(~has_prev)
    def _():
        clear(0)

    @pl.when(~has_next)
    def _():
        clear(5)

    get_w.wait()
    get_b.wait()
    for t in range(9):
        left, middle, right = (w_ref[3 * t + i] for i in range(3))
        tap = jnp.concatenate([middle, left, right, jnp.zeros_like(left)], axis=0)
        matrix[chans * t : chans * (t + 1)] = tap.T

    bias = b_ref[...].astype(jnp.float32)

    def compute(k):
        step_rows = ends[k] - begins[k]
        m = step_rows * cols
        place = lax.rem(lax.broadcasted_iota(jnp.int32, (m, 2 * outs), 0), cols)

        @pl.loop(0, 4)
        def _(z):
            windows = [
                x[z + dz, pl.ds(begins[k] + dy, step_rows)].reshape(m, chans)
                for dz in range(3)
                for dy in range(3)
            ]
            total = jnp.dot(
                jnp.concatenate(windows, axis=1), matrix[...], preferred_element_type=jnp.float32
            )
            near = total[:, : 2 * outs]
            far = total[:, 2 * outs :]
            before = jnp.where(place == 0, 0.0, pltpu.roll(near, 1, 0))
            after = jnp.where(place == cols - 1, 0.0, pltpu.roll(far, m - 1, 0))
            full = near + after + pltpu.roll(before, outs, 1)
            shifted = full[:, :outs] + bias
            result = jnp.where(shifted > 0, shifted, 0.3 * shifted)
            out_ref[z, pl.ds(begins[k], step_rows)] = result.astype(out_ref.dtype).reshape(
                step_rows, cols, outs
            )

    for t in range(CHUNKS + 2):
        k = t
        if k < CHUNKS:
            arrived(across + 1, k)
            c_fwd(k).start()

            @pl.when(~outer & sends_halo)
            def _():
                c_halo_fwd(k).start()

        k = t - 1
        if 0 <= k < CHUNKS:

            @pl.when(takes_halo)
            def _():
                arrived(halo_slot_in, k)
                c_halo_mate(k).start()

        k = t - 2
        if 0 <= k < CHUNKS:
            c_local(k).wait()
            arrived(mate + 1, k)
            arrived(diag + 1, k)

            @pl.when(mate_halo)
            def _():
                arrived(mate_slot, k)

            compute(k)

    for k in range(CHUNKS):
        c_y(k).wait_send()
        c_core(k).wait_send()
        c_fwd(k).wait_send()

        @pl.when(sends_halo)
        def _():
            c_halo_fwd(k).wait_send()

        @pl.when(takes_halo)
        def _():
            c_halo_mate(k).wait_send()


def body(volume, weights, bias):
    planes, rows, cols, chans = volume.shape
    outs = weights.shape[0]
    slabs = lax.axis_size("slab")
    depth = planes * lax.axis_size("filt")
    taps = weights.transpose(1, 0, 2)
    return pl.pallas_call(
        functools.partial(kernel, slabs),
        out_shape=pltpu.VMEM((depth, rows, cols, outs), jnp.bfloat16),
        in_specs=[
            pl.BlockSpec(memory_space=pltpu.HBM),
            pl.BlockSpec(memory_space=pltpu.HBM),
            pl.BlockSpec(memory_space=pltpu.HBM),
        ],
        out_specs=pl.BlockSpec(memory_space=pltpu.VMEM),
        scratch_shapes=[
            pltpu.VMEM((depth + 2, rows + 2, cols, chans), jnp.bfloat16),
            pltpu.VMEM((9 * chans, 4 * outs), jnp.bfloat16),
            pltpu.VMEM(taps.shape, jnp.bfloat16),
            pltpu.VMEM((1, outs), jnp.bfloat16),
            pltpu.SemaphoreType.DMA((5, CHUNKS)),
            pltpu.SemaphoreType.DMA((6, CHUNKS)),
            pltpu.SemaphoreType.DMA((CHUNKS,)),
            pltpu.SemaphoreType.DMA((2,)),
        ],
        compiler_params=pltpu.CompilerParams(
            collective_id=0, has_side_effects=True, vmem_limit_bytes=50 * 1024 * 1024
        ),
        cost_estimate=pl.CostEstimate(
            flops=2 * depth * rows * cols * outs * 27 * chans,
            bytes_accessed=16 * rows * cols * chans,
            transcendentals=0,
        ),
    )(volume, taps, bias.reshape(1, outs))


def solution(mesh):
    return jax.shard_map(
        body,
        mesh=mesh,
        in_specs=(P(("vol", "slab", "filt"), None, None, None), P("filt", None, None), P("filt")),
        out_specs=P(("vol", "slab"), None, None, "filt"),
        check_vma=False,
    )
```
